32 devices in a mesh: dp: 4 (over z), row: 4 (over y, x), col: 2 (over core).
Axes of the slice: x: 2, y: 2, z: 4, core: 2. Of those that a mesh axis runs over, the one named last changes fastest.
Arguments:
- hidden: bfloat16 [8192, 2048], P(('dp', 'row'), 'col'), may hold values from -6 to 6
- lengths: int32 [8], P('dp'), may hold values from 256 to 1024, as said below
- norm_gain: float32 [2048], P('col'), may hold values from 0.5 to 1.5
- w_gate: bfloat16 [2048, 4096], P('col', 'row'), may hold values from -0.125 to 0.125
- w_value: bfloat16 [2048, 4096], P('col', 'row'), may hold values from -0.125 to 0.125
- w_step: bfloat16 [2048, 64], P('col', 'row'), may hold values from -0.125 to 0.125
- w_state: bfloat16 [2048, 256], P('col'), may hold values from -0.125 to 0.125
- value_taps: float32 [4, 4096], P(None, ('row', 'col')), may hold values from -3 to 3
- value_shift: float32 [4096], P(('row', 'col')), may hold values from -3 to 3
- state_taps: float32 [4, 256], replicated, may hold values from -3 to 3
- state_shift: float32 [256], replicated, may hold values from -3 to 3
- step_bias: float32 [64], P(('row', 'col')), may hold values from -6 to -2.5
- decay_log: float32 [64], P(('row', 'col')), may hold values from 0 to 2.7
- skip_gain: float32 [64], P(('row', 'col')), may hold values from 0.5 to 1.5
- gated_gain: float32 [4096], P(('row', 'col')), may hold values from 0.5 to 1.5
- w_output: bfloat16 [4096, 2048], P('row', 'col'), may hold values from -0.09375 to 0.09375
- cotangent: bfloat16 [8192, 2048], P(('dp', 'row'), 'col'), may hold values from -6 to 6
Outputs:
- mixed: bfloat16 [8192, 2048], P(('dp', 'row'), 'col')
- grad_hidden: float32 [8192, 2048], P(('dp', 'row'), 'col')
- grad_norm_gain: float32 [2048], P('col')
- grad_w_gate: float32 [2048, 4096], P('col', 'row')
- grad_w_value: float32 [2048, 4096], P('col', 'row')
- grad_w_step: float32 [2048, 64], P('col', 'row')
- grad_w_state: float32 [2048, 256], P('col')
- grad_value_taps: float32 [4, 4096], P(None, ('row', 'col'))
- grad_value_shift: float32 [4096], P(('row', 'col'))
- grad_state_taps: float32 [4, 256], replicated
- grad_state_shift: float32 [256], replicated
- grad_step_bias: float32 [64], P(('row', 'col'))
- grad_decay_log: float32 [64], P(('row', 'col'))
- grad_skip_gain: float32 [64], P(('row', 'col'))
- grad_gated_gain: float32 [4096], P(('row', 'col'))
- grad_w_output: float32 [4096, 2048], P('row', 'col')
The draws below stay inside these ranges and needn't reach their ends.
Inputs may be any that keep to these rules, and one draw needn't show every extreme that they name: lengths[b] is the number of valid leading slots of sequence b; some sequence has exactly 1024 and some exactly 256.
All inputs are finite; a program needn't handle non-finite values.
Results may differ from the reference program's by a relative error of at most 0.008.
Values may be sent and summed in bfloat16 or wider, within the bound.
No kernel may reach another device: no remote copies, remote signals or barrier semaphores. Data moves between devices by JAX's collectives and lax.ppermute only.
A program may use at most 192 MiB of HBM per device.

```python
import math
import jax
import jax.numpy as jnp
from jax import lax

D = 2048
H = 64
N = 128
KW = 4
SPAN = 256
L = 1024
LMIN = 256
DI = 4096
SEQS = 8
TOKENS = 8192


def draw_lengths(key, part):
    drawn = jax.random.randint(key, (SEQS,), LMIN, L + 1, dtype=jnp.int32)
    drawn = drawn.at[0].set(L)
    return drawn.at[SEQS - 1].set(LMIN)


def steps_of(key, extent, shards, low, top_value):
    loudness = 1.0
    for axis_at, shards_of in shards:
        steps = jax.random.uniform(jax.random.fold_in(jax.random.fold_in(key, 6), axis_at), (shards_of,), jnp.float32, low / len(shards), top_value / len(shards))
        loudness = loudness * jnp.repeat(jnp.exp(steps), extent[axis_at] // shards_of).reshape((-1,) + (1,) * (len(extent) - 1 - axis_at))
    return loudness


def bell_draw(key, shape, deviation, most, shards=(), held_as=jnp.bfloat16):
    values = deviation * jax.random.normal(key, shape, jnp.float32)
    if shards:
        values = values * steps_of(key, shape, shards, -0.22, 0.18)
    return jnp.clip(values, -most, most).astype(held_as)


def setup_inputs(seed: int = 0) -> dict:
    arg_keys = jax.random.split(jax.random.key(seed), 18)
    return {
        "hidden": bell_draw(arg_keys[0], (TOKENS, D), 1.0, 6.0, ((0, 16), (1, 2))),
        "lengths": draw_lengths(jax.random.fold_in(arg_keys[17], 71), 0),
        "norm_gain": jnp.clip(1.0 + 0.1 * jax.random.normal(arg_keys[2], (D,), jnp.float32), 0.5, 1.5),
        "w_gate": bell_draw(arg_keys[3], (D, DI), D ** -0.5, 0.125, ((0, 2), (1, 4))),
        "w_value": bell_draw(arg_keys[4], (D, DI), D ** -0.5, 0.125, ((0, 2), (1, 4))),
        "w_step": bell_draw(arg_keys[5], (D, H), D ** -0.5, 0.125, ((0, 2), (1, 4))),
        "w_state": bell_draw(arg_keys[6], (D, 2 * N), D ** -0.5, 0.125, ((0, 2),)),
        "value_taps": bell_draw(arg_keys[7], (KW, DI), KW ** -0.5, 3.0, ((1, 8),), jnp.float32),
        "value_shift": bell_draw(arg_keys[8], (DI,), 0.5, 3.0, ((0, 8),), jnp.float32),
        "state_taps": bell_draw(arg_keys[9], (KW, 2 * N), KW ** -0.5, 3.0, (), jnp.float32),
        "state_shift": bell_draw(arg_keys[10], (2 * N,), 0.5, 3.0, (), jnp.float32),
        "step_bias": jnp.clip(-6.0 + 3.5 * jax.random.uniform(arg_keys[11], (H,), jnp.float32) ** steps_of(arg_keys[11], (H,), ((0, 8),), -0.2, 0.2), -6.0, -2.5),
        "decay_log": jnp.clip(2.7 * jax.random.uniform(arg_keys[12], (H,), jnp.float32) ** steps_of(arg_keys[12], (H,), ((0, 8),), -0.2, 0.2), 0.0, 2.7),
        "skip_gain": jnp.clip(0.5 + 1.0 * jax.random.uniform(arg_keys[13], (H,), jnp.float32) ** steps_of(arg_keys[13], (H,), ((0, 8),), -0.2, 0.2), 0.5, 1.5),
        "gated_gain": jnp.clip(1.0 + 0.1 * jax.random.normal(arg_keys[14], (DI,), jnp.float32), 0.5, 1.5),
        "w_output": bell_draw(arg_keys[15], (DI, D), DI ** -0.5, 0.09375, ((0, 4), (1, 2))),
        "cotangent": bell_draw(arg_keys[16], (TOKENS, D), 1.0, 6.0, ((0, 16), (1, 2))),
    }


@jax.custom_vjp
def low(v):
    return lax.optimization_barrier(v.astype(jnp.bfloat16)).astype(jnp.float32)

@jax.custom_vjp
def low_back(v):
    return v

def low_keep(v):
    return (low(v), None)

def low_pass(kept, grad):
    return (grad,)

def back_keep(v):
    return (v, None)

def back_low(kept, grad):
    return (low(grad),)
low.defvjp(low_keep, low_pass)
low_back.defvjp(back_keep, back_low)
EPS = 1e-05
exact_prec = lax.Precision.HIGHEST

def causal_conv(values, kernel_taps, shift_bias):
    tap_count = kernel_taps.shape[0]
    seq_len = values.shape[1]
    padded = jnp.pad(values, ((0, 0), (tap_count - 1, 0), (0, 0)))
    result = shift_bias + jnp.zeros_like(values)
    for offset in range(tap_count):
        result = result + kernel_taps[offset] * padded[:, offset:offset + seq_len, :]
    return result

def ssd_scan(values, step_size, decay_rate, write_vec, read_vec, block_len):
    seq_count, seq_len, head_count, head_dim = values.shape
    state_dim = write_vec.shape[2]
    block_count = seq_len // block_len
    lower_tri = jnp.arange(block_len)[:, None] >= jnp.arange(block_len)[None, :]

    def split_blocks(tensor):
        shaped = tensor.reshape((seq_count, block_count, block_len) + tensor.shape[2:])
        return jnp.moveaxis(shaped, 1, 0)

    def advance(carry_state, pieces):
        block_vals, block_steps, block_write, block_read = pieces
        cum_decay = jnp.cumsum(block_steps * decay_rate, axis=1)
        pair_diff = cum_decay[:, :, None, :] - cum_decay[:, None, :, :]
        lower_mask = lower_tri[None, :, :, None]
        pair_decay = jnp.where(lower_mask, jnp.exp(jnp.where(lower_mask, pair_diff, 0.0)), 0.0)
        read_write = jnp.einsum('stn,sun->stu', block_read, block_write, precision=exact_prec)
        mix_weights = read_write[..., None] * pair_decay * block_steps[:, None, :, :]
        within = jnp.einsum('stuh,suhp->sthp', mix_weights, block_vals, precision=exact_prec)
        carried = jnp.einsum('stn,shpn->sthp', block_read, carry_state, precision=exact_prec)
        carried = carried * jnp.exp(cum_decay)[..., None]
        tail_weight = jnp.exp(cum_decay[:, -1:, :] - cum_decay) * block_steps
        update = jnp.einsum('suhp,sun->shpn', tail_weight[..., None] * block_vals, block_write, precision=exact_prec)
        new_state = carry_state * jnp.exp(cum_decay[:, -1, :])[:, :, None, None] + update
        return (new_state, within + carried)
    start_state = jnp.zeros((seq_count, head_count, head_dim, state_dim), values.dtype)
    final_state, block_outs = lax.scan(jax.checkpoint(advance), start_state, (split_blocks(values), split_blocks(step_size), split_blocks(write_vec), split_blocks(read_vec)))
    return jnp.moveaxis(block_outs, 0, 1).reshape(values.shape)

def layer_forward(params, hidden_rows, mask_rows, seq_count):
    norm_gain, w_gate, w_value, w_step, w_state, value_taps, value_shift, state_taps, state_shift, step_bias, decay_log, skip_gain, gated_gain, w_output = params
    inner_dim = w_gate.shape[1]
    head_count = w_step.shape[1]
    state_dim = w_state.shape[1] // 2
    square_mean = lax.optimization_barrier(jnp.mean(hidden_rows * hidden_rows, axis=1))
    inv_scale = lax.rsqrt(square_mean + EPS)
    normed = low(hidden_rows * norm_gain)
    weight_in = jnp.concatenate([w_gate, w_value, w_step, w_state], axis=1)
    project = low_back(jnp.dot(normed, weight_in, precision=exact_prec))
    scaled = inv_scale[:, None] * project
    gate_pre = scaled[:, :inner_dim]
    value_pre = scaled[:, inner_dim:2 * inner_dim]
    step_pre = scaled[:, 2 * inner_dim:2 * inner_dim + head_count]
    state_pre = scaled[:, 2 * inner_dim + head_count:]
    conv_in = jnp.concatenate([value_pre, state_pre], axis=1).reshape(seq_count, -1, inner_dim + 2 * state_dim)
    seq_len = conv_in.shape[1]
    conv_out = jax.nn.silu(causal_conv(conv_in, jnp.concatenate([value_taps, state_taps], axis=1), jnp.concatenate([value_shift, state_shift])))
    values = conv_out[..., :inner_dim].reshape(seq_count, seq_len, head_count, -1)
    write_vec = conv_out[..., inner_dim:inner_dim + state_dim]
    read_vec = conv_out[..., inner_dim + state_dim:]
    mask_seq = mask_rows.reshape(seq_count, seq_len)
    step_size = jax.nn.softplus(step_pre.reshape(seq_count, seq_len, head_count) + step_bias) * mask_seq[..., None]
    decay_rate = -jnp.exp(decay_log)
    mixed_y = ssd_scan(values, step_size, decay_rate, write_vec, read_vec, SPAN) + skip_gain[:, None] * values
    mixed_y = mixed_y * mask_seq[..., None, None]
    gated = mixed_y.reshape(-1, inner_dim) * jax.nn.silu(gate_pre)
    inv_gate = lax.rsqrt(lax.optimization_barrier(jnp.mean(gated * gated, axis=1)) + EPS)
    normal_out = low(gated * inv_gate[:, None] * gated_gain)
    return hidden_rows + jnp.dot(normal_out, w_output, precision=exact_prec)

def reference(hidden, lengths, norm_gain, w_gate, w_value, w_step, w_state, value_taps, value_shift, state_taps, state_shift, step_bias, decay_log, skip_gain, gated_gain, w_output, cotangent):
    params = jax.tree.map(lambda tensor: tensor.astype(jnp.float32), (norm_gain, w_gate, w_value, w_step, w_state, value_taps, value_shift, state_taps, state_shift, step_bias, decay_log, skip_gain, gated_gain, w_output))
    group_seqs = math.gcd(SEQS, max(1, 4096 // L))
    block_count = SEQS // group_seqs
    block_rows = group_seqs * L
    hidden_blocks = hidden.astype(jnp.float32).reshape(block_count, block_rows, D)
    cot_blocks = cotangent.astype(jnp.float32).reshape(block_count, block_rows, D)
    slot_pos = jnp.arange(L, dtype=jnp.int32)
    mask_blocks = (slot_pos[None, :] < lengths.astype(jnp.int32)[:, None]).astype(jnp.float32)
    mask_blocks = mask_blocks.reshape(block_count, block_rows)

    def per_block(totals, pieces):
        hidden_in, mask_in, cot_in = pieces

        def run_block(params_in, rows_in):
            return layer_forward(params_in, rows_in, mask_in, group_seqs)
        block_out, pullback = jax.vjp(run_block, params, hidden_in)
        grad_params, hidden_grad = pullback(cot_in)
        totals = jax.tree.map(jnp.add, totals, grad_params)
        return (totals, (block_out, hidden_grad))
    zeros = jax.tree.map(jnp.zeros_like, params)
    totals, (mixed_blocks, grad_blocks) = lax.scan(per_block, zeros, (hidden_blocks, mask_blocks, cot_blocks))
    mixed = mixed_blocks.reshape(TOKENS, D).astype(jnp.bfloat16)
    grad_hidden = grad_blocks.reshape(TOKENS, D)
    return (mixed, grad_hidden, totals[0], totals[1], totals[2], totals[3], totals[4], totals[5], totals[6], totals[7], totals[8], totals[9], totals[10], totals[11], totals[12], totals[13])
```

```python
import functools

import jax
import jax.numpy as jnp
from jax import lax
from jax.experimental import pallas as pl
from jax.experimental.pallas import tpu as pltpu
from jax.sharding import PartitionSpec as P

EPS = 1e-05
CHUNK = 128
BLOCK = 256
LANES = 128
F32 = jnp.float32
BF16 = jnp.bfloat16
HIGH = lax.Precision.HIGHEST
NN = (((1,), (0,)), ((), ()))
NT = (((1,), (1,)), ((), ()))
TN = (((0,), (0,)), ((), ()))
VMEM_BYTES = 56 * 1024 * 1024


def mm(a, b, dims):
    return lax.dot_general(a, b, dims, preferred_element_type=F32)


def mm_exact(a, b):
    return lax.dot_general(a, b, NN, precision=HIGH, preferred_element_type=F32)


def sigmoid(u):
    return 1.0 / (1.0 + jnp.exp(-u))


def softplus(u):
    return jnp.maximum(u, 0.0) + jnp.log1p(jnp.exp(-jnp.abs(u)))


def iota(shape, dim):
    return lax.broadcasted_iota(jnp.int32, shape, dim)


def forward_kernel(heads, len_ref, xa, xb, ga, gb, wga, wgb, wva, wvb, wsa, wsb, pch, phd,
                   o_na, o_gate, o_vpre, o_vconv, o_y, o_spre, o_sconv, o_sp, o_sin, o_g, o_stats,
                   cat, state):
    inner = wgb.shape[1]
    state_dim = o_spre.shape[1] // 2
    blocks = pl.num_programs(1)
    blk = pl.program_id(1)
    length = len_ref[pl.program_id(0)]
    model = xa.shape[1] + xb.shape[1]

    @pl.when(blk == 0)
    def _():
        cat[0:8, :] = jnp.zeros((8, cat.shape[1]), F32)
        state[...] = jnp.zeros_like(state)

    @pl.when(blk > 0)
    def _():
        cat[0:8, :] = cat[BLOCK : BLOCK + 8, :]

    a32 = xa[...].astype(F32)
    b32 = xb[...].astype(F32)
    square = jnp.sum(a32 * a32, axis=1, keepdims=True) + jnp.sum(b32 * b32, axis=1, keepdims=True)
    inv = lax.rsqrt(square / model + EPS)
    na = (a32 * ga[...]).astype(BF16)
    nb = (b32 * gb[...]).astype(BF16)
    o_na[...] = na
    gate = inv * (mm(na, wga[...], NN) + mm(nb, wgb[...], NN))
    o_gate[...] = gate
    vpre = inv * (mm(na, wva[...], NN) + mm(nb, wvb[...], NN))
    o_vpre[...] = vpre
    small = inv * (mm(na, wsa[...], NN) + mm(nb, wsb[...], NN))
    spre = small[:, : 2 * state_dim]
    o_spre[...] = spre
    sp = small[:, 2 * state_dim :] + phd[0:1, :]
    o_sp[...] = sp
    cat[8 : 8 + BLOCK, :inner] = vpre
    cat[8 : 8 + BLOCK, inner:] = spre
    conv = pch[4:5, :] + pch[0:1, :] * cat[5 : 5 + BLOCK, :]
    for k in range(1, 4):
        conv = conv + pch[k : k + 1, :] * cat[5 + k : 5 + k + BLOCK, :]
    o_vconv[...] = conv[:, :inner]
    o_sconv[...] = conv[:, inner:]
    act = conv * sigmoid(conv)
    pos = blk * BLOCK + iota((BLOCK, 1), 0)
    mask = (pos < length).astype(F32)
    step = softplus(sp) * mask
    lower = iota((CHUNK, CHUNK), 0) >= iota((CHUNK, CHUNK), 1)
    lower_f = lower.astype(F32)
    left = iota((CHUNK, LANES), 1) < (LANES // 2)
    gated_parts = []
    for ch in range(BLOCK // CHUNK):
        rows = slice(ch * CHUNK, (ch + 1) * CHUNK)
        o_sin[ch] = state[...].astype(BF16)
        stp = step[rows]
        cum = mm_exact(lower_f, stp * phd[1:2, :])
        cum_t = cum.T
        write = act[rows, inner : inner + state_dim].astype(BF16)
        read = act[rows, inner + state_dim :].astype(BF16)
        scores = mm(read, write, NT)
        carried = mm(read, state[...].astype(BF16), NN)
        tails = []
        decays = []
        for pair in range(heads // 2):
            lanes = slice(pair * LANES, (pair + 1) * LANES)
            vals = act[rows, lanes]
            weights = []
            bcs = []
            sbs = []
            for h in (2 * pair, 2 * pair + 1):
                bc = jnp.broadcast_to(cum[:, h : h + 1], (CHUNK, CHUNK))
                diff = bc - cum_t[h : h + 1, :]
                weights.append((scores * jnp.exp(jnp.where(lower, diff, -1e30))).astype(BF16))
                bcs.append(bc)
                sbs.append(jnp.broadcast_to(stp[:, h : h + 1], (CHUNK, LANES)))
            cum_p = jnp.where(left, bcs[0], bcs[1])
            dval = vals * jnp.where(left, sbs[0], sbs[1])
            dlow = dval.astype(BF16)
            zero = jnp.zeros_like(dlow)
            stacked = jnp.concatenate([jnp.where(left, dlow, zero), jnp.where(left, zero, dlow)], axis=0)
            within = mm(jnp.concatenate(weights, axis=1), stacked, NN)
            last = cum_p[CHUNK - 1 : CHUNK, :]
            scan_out = within + carried[:, lanes] * jnp.exp(cum_p)
            tails.append((dval * jnp.exp(last - cum_p)).astype(BF16))
            decays.append(jnp.exp(last))
            y = (scan_out + pch[5:6, lanes] * vals) * mask[rows]
            o_y[rows, lanes] = y
        decay = decays[0] if len(decays) == 1 else jnp.concatenate(decays, axis=1)
        tail = tails[0] if len(tails) == 1 else jnp.concatenate(tails, axis=1)
        state[...] = state[...] * decay + mm(write, tail, TN)
    gated = o_y[...] * (gate * sigmoid(gate))
    o_g[...] = (gated * pch[6:7, :inner]).astype(BF16)
    gate_square = jnp.sum(gated * gated, axis=1, keepdims=True)
    lane = iota((BLOCK, LANES), 1)
    stats = jnp.where(lane == 0, gate_square, jnp.where(lane == 1, inv, 0.0))
    o_stats[...] = stats.T[0:8, :]


def run_forward(heads, lens_col, xa, xb, ga, gb, wg, wgb, wv, wvb, wsa, wsb, pch, phd, seqs):
    tokens, part = xa.shape
    inner = wgb.shape[1]
    sd2 = pch.shape[1] - inner
    per_seq = tokens // seqs // BLOCK
    chunks = BLOCK // CHUNK
    tok = lambda width: pl.BlockSpec((BLOCK, width), lambda s, i, p: (s * per_seq + i, 0))
    whole = lambda shape: pl.BlockSpec(shape, lambda s, i, p: (0,) * len(shape))
    own = pl.BlockSpec((part, inner), lambda s, i, p: (0, p[seqs]))
    sds = jax.ShapeDtypeStruct
    return pl.pallas_call(
        functools.partial(forward_kernel, heads),
        out_shape=[
            sds((tokens, part), BF16),
            sds((tokens, inner), F32),
            sds((tokens, inner), F32),
            sds((tokens, inner), F32),
            sds((tokens, inner), F32),
            sds((tokens, sd2), F32),
            sds((tokens, sd2), F32),
            sds((tokens, LANES), F32),
            sds((tokens // CHUNK, sd2 // 2, inner), BF16),
            sds((tokens, inner), BF16),
            sds((8, tokens), F32),
        ],
        grid_spec=pltpu.PrefetchScalarGridSpec(
            num_scalar_prefetch=1,
            grid=(seqs, per_seq),
            in_specs=[
                tok(part), tok(part), whole((1, part)), whole((1, part)),
                own, whole((part, inner)), own, whole((part, inner)),
                whole(wsa.shape), whole(wsb.shape), whole(pch.shape), whole(phd.shape),
            ],
            out_specs=[
                tok(part), tok(inner), tok(inner), tok(inner), tok(inner), tok(sd2), tok(sd2), tok(LANES),
                pl.BlockSpec((chunks, sd2 // 2, inner), lambda s, i, p: (s * per_seq + i, 0, 0)),
                tok(inner),
                pl.BlockSpec((8, BLOCK), lambda s, i, p: (0, s * per_seq + i)),
            ],
            scratch_shapes=[
                pltpu.VMEM((BLOCK + 8, inner + sd2), F32),
                pltpu.VMEM((sd2 // 2, inner), F32),
            ],
        ),
        compiler_params=pltpu.CompilerParams(
            dimension_semantics=("arbitrary", "arbitrary"), vmem_limit_bytes=VMEM_BYTES
        ),
        name="ssd_forward",
        cost_estimate=pl.CostEstimate(
            flops=2 * tokens * 2 * part * (2 * inner + wsa.shape[1]), bytes_accessed=tokens * inner * 24,
            transcendentals=tokens * inner * 4),
    )(lens_col, xa, xb, ga, gb, wg, wgb, wv, wvb, wsa, wsb, pch, phd)


def back_norm_kernel(c_ref, ca, cb, wa, wb, g, o_bn, o_stats):
    bn = mm(ca[...], wa[...], NT) + mm(cb[...], wb[...], NT)
    o_bn[...] = bn
    total = jnp.sum(bn * g[...].astype(F32), axis=1, keepdims=True)
    o_stats[...] = jnp.broadcast_to(total, (total.shape[0], LANES)).T[0:8, :]


def run_back_norm(col, cot_a, cot_b, w_out, w_out_b, g):
    tokens, part = cot_a.shape
    inner = g.shape[1]
    tok = lambda width: pl.BlockSpec((BLOCK, width), lambda i, p: (i, 0))
    return pl.pallas_call(
        back_norm_kernel,
        out_shape=[jax.ShapeDtypeStruct((tokens, inner), F32), jax.ShapeDtypeStruct((8, tokens), F32)],
        grid_spec=pltpu.PrefetchScalarGridSpec(
            num_scalar_prefetch=1,
            grid=(tokens // BLOCK,),
            in_specs=[
                tok(part), tok(part),
                pl.BlockSpec((inner, part), lambda i, p: (p[0], 0)),
                pl.BlockSpec((inner, part), lambda i, p: (0, 0)),
                tok(inner),
            ],
            out_specs=[tok(inner), pl.BlockSpec((8, BLOCK), lambda i, p: (0, i))],
        ),
        compiler_params=pltpu.CompilerParams(dimension_semantics=("arbitrary",), vmem_limit_bytes=VMEM_BYTES),
        name="back_norm",
        cost_estimate=pl.CostEstimate(flops=4 * tokens * part * inner, bytes_accessed=tokens * part * 8, transcendentals=0),
    )(col, cot_a, cot_b, w_out, w_out_b, g)


def fold8(t):
    return jnp.sum(t.reshape(t.shape[0] // 8, 8, t.shape[1]), axis=0)


def backward_kernel(heads, len_ref, rows8, bn, gate_r, vpre_r, vconv_r, y_r, spre_r, sconv_r, sp_r, sin_r, pch, phd, seg,
                    o_dg, o_dv, o_ds, o_pc, o_ph, dcat, dstate):
    inner = bn.shape[1]
    sd = sconv_r.shape[1] // 2
    i = pl.program_id(1)
    chunks = pl.num_programs(1)
    length = len_ref[pl.program_id(0)]

    @pl.when((i == 0) & (pl.program_id(0) == 0))
    def _():
        o_pc[...] = jnp.zeros_like(o_pc)
        o_ph[...] = jnp.zeros_like(o_ph)

    @pl.when(i == 0)
    def _():
        dcat[CHUNK : CHUNK + 8, :] = jnp.zeros((8, dcat.shape[1]), F32)
        dstate[...] = jnp.zeros_like(dstate)

    @pl.when(i > 0)
    def _():
        dcat[CHUNK : CHUNK + 8, :] = dcat[0:8, :]

    cols = jnp.concatenate([rows8[...], jnp.zeros((LANES - 8, CHUNK), F32)], axis=0).T
    ig, c2, isc = cols[:, 0:1], cols[:, 1:2], cols[:, 2:3]
    pos = (chunks - 1 - i) * CHUNK + iota((CHUNK, 1), 0)
    mask = (pos < length).astype(F32)
    gate = gate_r[...]
    y = y_r[...]
    sg = sigmoid(gate)
    sil = gate * sg
    gated = y * sil
    back = bn[...]
    gb = ig * pch[6:7, :inner] * back - c2 * gated
    o_pc[48:56, :inner] += fold8(back * gated * ig)
    dy = gb * sil * mask
    o_dg[...] = (isc * (gb * y * (sg * (1.0 + gate * (1.0 - sg))))).astype(BF16)
    vconv = vconv_r[...]
    sgv = sigmoid(vconv)
    vals = vconv * sgv
    o_pc[40:48, :inner] += fold8(dy * vals)
    sconv = sconv_r[...]
    sgs = sigmoid(sconv)
    sact = (sconv * sgs).astype(BF16)
    write, read = sact[:, :sd], sact[:, sd:]
    sp = sp_r[...]
    step = softplus(sp) * mask
    row_i, col_i = iota((CHUNK, CHUNK), 0), iota((CHUNK, CHUNK), 1)
    lower = row_i >= col_i
    left = col_i < (LANES // 2)
    cum = mm_exact(lower.astype(F32), step * phd[1:2, :])
    cum_t = cum.T
    step_t = step.T
    scores = mm(read, write, NT)
    s_in = sin_r[0]
    ds = dstate[...]
    ds_low = ds.astype(BF16)
    read_s = mm(read, s_in, NN)
    write_s = mm(write, ds_low, NN)
    dscores = jnp.zeros((CHUNK, CHUNK), F32)
    row_sums = jnp.zeros((CHUNK, LANES), F32)
    col_rows = []
    x1s, x2s, us, zs, decays = [], [], [], [], []
    for pair in range(heads // 2):
        lanes = slice(pair * LANES, (pair + 1) * LANES)
        dy_p = dy[:, lanes]
        v_p = vals[:, lanes]
        dlow = dy_p.astype(BF16)
        zero = jnp.zeros_like(dlow)
        dstack = jnp.concatenate([jnp.where(left, dlow, zero), jnp.where(left, zero, dlow)], axis=0)
        dmix = mm(dstack, v_p.astype(BF16), NT)
        bcs, sbs, weights = [], [], []
        for e in range(2):
            h = 2 * pair + e
            bc = jnp.broadcast_to(cum[:, h : h + 1], (CHUNK, CHUNK))
            decay = jnp.exp(jnp.where(lower, bc - cum_t[h : h + 1, :], -1e30))
            srow = step_t[h : h + 1, :]
            t1 = dmix[e * CHUNK : (e + 1) * CHUNK, :] * decay
            e1 = t1 * scores
            col_rows.append(jnp.sum(e1, axis=0, keepdims=True))
            row_sums = jnp.where(col_i == h, jnp.sum(e1 * srow, axis=1, keepdims=True), row_sums)
            dscores = dscores + t1 * srow
            weights.append((scores * decay * srow).astype(BF16))
            bcs.append(bc)
            sbs.append(jnp.broadcast_to(step[:, h : h + 1], (CHUNK, LANES)))
        dv_in = mm(jnp.concatenate(weights, axis=0), dstack, TN)
        cum_p = jnp.where(left, bcs[0], bcs[1])
        step_p = jnp.where(left, sbs[0], sbs[1])
        last = cum_p[CHUNK - 1 : CHUNK, :]
        tail = jnp.exp(last - cum_p)
        x1 = dy_p * jnp.exp(cum_p)
        tz = tail * write_s[:, lanes]
        x1s.append(x1.astype(BF16))
        x2s.append((step_p * tail * v_p).astype(BF16))
        us.append(x1 * read_s[:, lanes])
        zs.append(v_p * tz)
        decays.append(jnp.exp(last))
        dvt = pch[5:6, lanes] * dy_p + dv_in + step_p * tz
        sg_p = sgv[:, lanes]
        dcat[0:CHUNK, lanes] = dvt * (sg_p * (1.0 + vconv[:, lanes] * (1.0 - sg_p)))
    join = lambda parts: parts[0] if len(parts) == 1 else jnp.concatenate(parts, axis=1)
    x1, x2, u_all, z_all, decay = join(x1s), join(x2s), join(us), join(zs), join(decays)
    ds_bf = dscores.astype(BF16)
    dread = mm(x1, s_in, NT) + mm(ds_bf, write, NN)
    dwrite = mm(x2, ds_low, NT) + mm(ds_bf, read, TN)
    dsil_s = sgs * (1.0 + sconv * (1.0 - sgs))
    dcat[0:CHUNK, inner : inner + sd] = dwrite * dsil_s[:, :sd]
    dcat[0:CHUNK, inner + sd :] = dread * dsil_s[:, sd:]
    kap = jnp.sum(s_in.astype(F32) * ds, axis=0, keepdims=True) * decay
    stacked = jnp.concatenate([u_all, z_all, jnp.broadcast_to(kap, (8, inner))], axis=0)
    hi = stacked.astype(BF16)
    lo = (stacked - hi.astype(F32)).astype(BF16)
    sums = mm(hi, seg[...], NN) + mm(lo, seg[...], NN)
    u_h, z_h, kap_h = sums[:CHUNK], sums[CHUNK : 2 * CHUNK], sums[2 * CHUNK : 2 * CHUNK + 1]
    dstate[...] = ds * decay + mm(read, x1, TN)
    col_rows.append(jnp.zeros((LANES - heads, CHUNK), F32))
    col_sums = jnp.concatenate(col_rows, axis=0).T
    dcum = row_sums - step * col_sums + u_h
    upper_f = (row_i <= col_i).astype(F32)
    strict_f = (row_i > col_i).astype(F32)
    da = mm_exact(upper_f, dcum) + mm_exact(strict_f, step * z_h) + kap_h
    dstep = col_sums + z_h + phd[1:2, :] * da
    o_ph[8:16, :] += fold8(step * da)
    dsp = dstep * mask * sigmoid(sp)
    o_ph[0:8, :] += fold8(dsp)
    taps = pch[0:4, :]
    din = jnp.zeros((CHUNK, inner + 2 * sd), F32)
    ins = jnp.concatenate([vpre_r[...], spre_r[...]], axis=1)
    for k in range(4):
        shifted = dcat[3 - k : 3 - k + CHUNK, :]
        din = din + taps[k : k + 1, :] * shifted
        o_pc[8 * k : 8 * k + 8, :] += fold8(shifted * ins)
    o_pc[32:40, :] += fold8(dcat[0:CHUNK, :])
    dlow = (isc * din).astype(BF16)
    o_dv[...] = dlow[:, :inner]
    o_ds[:, : 2 * sd] = dlow[:, inner:]
    o_ds[:, 2 * sd :] = (isc * dsp).astype(BF16)


def run_backward(heads, lens_col, rows8, bn, gate, vpre, vconv, y, spre, sconv, sp, sin, pch, phd, seg, seqs):
    tokens, inner = bn.shape
    sd2 = spre.shape[1]
    per_seq = tokens // seqs // CHUNK
    at = lambda s, i: s * per_seq + per_seq - 1 - i
    tok = lambda width: pl.BlockSpec((CHUNK, width), lambda s, i, p: (at(s, i), 0))
    whole = lambda shape: pl.BlockSpec(shape, lambda s, i, p: (0,) * len(shape))
    sds = jax.ShapeDtypeStruct
    return pl.pallas_call(
        functools.partial(backward_kernel, heads),
        out_shape=[
            sds((tokens, inner), BF16),
            sds((tokens, inner), BF16),
            sds((tokens, sd2 + LANES), BF16),
            sds((56, inner + sd2), F32),
            sds((16, LANES), F32),
        ],
        grid_spec=pltpu.PrefetchScalarGridSpec(
            num_scalar_prefetch=1,
            grid=(seqs, per_seq),
            in_specs=[
                pl.BlockSpec((8, CHUNK), lambda s, i, p: (0, at(s, i))),
                tok(inner), tok(inner), tok(inner), tok(inner), tok(inner), tok(sd2), tok(sd2), tok(LANES),
                pl.BlockSpec((1, sd2 // 2, inner), lambda s, i, p: (at(s, i), 0, 0)),
                whole(pch.shape), whole(phd.shape), whole(seg.shape),
            ],
            out_specs=[tok(inner), tok(inner), tok(sd2 + LANES), whole((56, inner + sd2)), whole((16, LANES))],
            scratch_shapes=[
                pltpu.VMEM((CHUNK + 8, inner + sd2), F32),
                pltpu.VMEM((sd2 // 2, inner), F32),
            ],
        ),
        compiler_params=pltpu.CompilerParams(
            dimension_semantics=("arbitrary", "arbitrary"), vmem_limit_bytes=VMEM_BYTES
        ),
        name="ssd_backward",
        cost_estimate=pl.CostEstimate(
            flops=tokens * inner * 4000, bytes_accessed=tokens * inner * 32, transcendentals=tokens * inner * 8),
    )(lens_col, rows8, bn, gate, vpre, vconv, y, spre, sconv, sp, sin, pch, phd, seg)


def input_back_kernel(s_ref, dgo, dgr, dvo, dvr, dso, dsr, xa, ga, wgo, wgr, wvo, wvr, wso, wsr, o_part, o_stats, o_gain):
    sd2 = dso.shape[1] - LANES
    so = dso[...]
    sr = dsr[...]
    both = (so[:, :sd2].astype(F32) + sr[:, :sd2].astype(F32)).astype(BF16)
    out = mm(dgo[...], wgo[...], NT) + mm(dgr[...], wgr[...], NT)
    out = out + mm(dvo[...], wvo[...], NT) + mm(dvr[...], wvr[...], NT)
    out = out + mm(both, wso[:, :sd2], NT) + mm(so[:, sd2:], wso[:, sd2:], NT) + mm(sr[:, sd2:], wsr[:, sd2:], NT)
    o_part[...] = out.astype(BF16)
    x32 = xa[...].astype(F32)
    normed = (x32 * ga[...]).astype(BF16).astype(F32)
    total = jnp.sum(out * normed, axis=1, keepdims=True)
    o_stats[...] = jnp.broadcast_to(total, (total.shape[0], LANES)).T[0:8, :]

    @pl.when(pl.program_id(0) == 0)
    def _():
        o_gain[...] = jnp.zeros_like(o_gain)

    o_gain[...] += fold8(out * x32)


def run_input_back(scal, tokens, dgo, dgr, dvo, dvr, dso, dsr, xa, ga, wg, wv, wso, wsr):
    part = xa.shape[1]
    inner = dgo.shape[1]
    block = min(BLOCK, tokens)
    tok = lambda width: pl.BlockSpec((block, width), lambda i, p: (p[0] + i, 0))
    whole = lambda shape: pl.BlockSpec(shape, lambda i, p: (0,) * len(shape))
    own = pl.BlockSpec((part, inner), lambda i, p: (0, p[1]))
    other = pl.BlockSpec((part, inner), lambda i, p: (0, p[2]))
    small = dso.shape[1]
    return pl.pallas_call(
        input_back_kernel,
        out_shape=[
            jax.ShapeDtypeStruct((tokens, part), BF16),
            jax.ShapeDtypeStruct((8, tokens), F32),
            jax.ShapeDtypeStruct((8, part), F32),
        ],
        grid_spec=pltpu.PrefetchScalarGridSpec(
            num_scalar_prefetch=1,
            grid=(tokens // block,),
            in_specs=[
                tok(inner), tok(inner), tok(inner), tok(inner), tok(small), tok(small), tok(part), whole((1, part)),
                own, other, own, other, whole(wso.shape), whole(wsr.shape),
            ],
            out_specs=[
                pl.BlockSpec((block, part), lambda i, p: (i, 0)),
                pl.BlockSpec((8, block), lambda i, p: (0, i)),
                whole((8, part)),
            ],
        ),
        compiler_params=pltpu.CompilerParams(dimension_semantics=("arbitrary",), vmem_limit_bytes=VMEM_BYTES),
        name="input_back",
        cost_estimate=pl.CostEstimate(
            flops=2 * tokens * part * (4 * inner + small), bytes_accessed=tokens * inner * 12, transcendentals=0),
    )(scal, dgo, dgr, dvo, dvr, dso, dsr, xa, ga, wg, wg, wv, wv, wso, wsr)


def swap_col(t):
    return lax.ppermute(t, "col", [(0, 1), (1, 0)])


def flip_row(t, bits):
    return lax.ppermute(t, "row", [(r, r ^ bits) for r in range(4)])


def gather_both(t, row, small_rows):
    count = lax.axis_size("row")
    rows, width = t.shape
    if not small_rows:
        mine = lax.all_gather(t, "row", axis=0, tiled=True)
        return mine, swap_col(mine)
    half = rows // 2
    near, far = flip_row(t, 1), flip_row(t, 2)
    low, high = flip_row(near[:half], 2), flip_row(far[half:], 1)
    mine = jnp.zeros((count * rows, width), t.dtype)
    theirs = jnp.zeros((count * rows, width), t.dtype)
    for piece, bits, shift in ((t, 0, 0), (near, 1, 0), (far, 2, 0), (low, 3, 0), (high, 3, half)):
        start = (row ^ bits) * rows + shift
        mine = lax.dynamic_update_slice(mine, piece, (start, 0))
        theirs = lax.dynamic_update_slice(theirs, swap_col(piece), (start, 0))
    return mine, theirs


def scatter_four(part_of, rows):
    half = rows // 2
    diag = part_of(3)
    low = flip_row(diag[:half], 1)
    high = flip_row(diag[half:], 2)
    far, near = part_of(2), part_of(1)
    far = jnp.concatenate([(far[:half].astype(F32) + low.astype(F32)).astype(BF16), far[half:]], axis=0)
    near = jnp.concatenate([near[:half], (near[half:].astype(F32) + high.astype(F32)).astype(BF16)], axis=0)
    got_far, got_near = flip_row(far, 2), flip_row(near, 1)
    return part_of(0).astype(F32) + got_far.astype(F32) + got_near.astype(F32)


def line_sum(t, axis):
    n = lax.axis_size(axis)
    if n == 1:
        return t.astype(BF16)
    me = lax.axis_index(axis)
    rows = t.shape[0] // n
    part = lambda k: lax.dynamic_slice_in_dim(t, jnp.clip(k, 0, n - 1) * rows, rows, 0).astype(F32)
    up = down = None
    for slot in range(1, n):
        send_up = part(n - slot + me)
        send_down = part(slot - n + me)
        if up is not None:
            send_up = send_up + up.astype(F32)
            send_down = send_down + down.astype(F32)
        up = lax.ppermute(send_up.astype(BF16), axis, [(i, i + 1) for i in range(min(slot, n - 1))])
        down = lax.ppermute(send_down.astype(BF16), axis, [(n - 1 - i, n - 2 - i) for i in range(min(slot, n - 1))])
    total = (part(me) + up.astype(F32) + down.astype(F32)).astype(BF16)
    up = down = total
    before, after = [], []
    for step in range(n - 1):
        up = lax.ppermute(up, axis, [(i, i + 1) for i in range(step, n - 1)])
        down = lax.ppermute(down, axis, [(n - 1 - i, n - 2 - i) for i in range(step, n - 1)])
        before.append(up)
        after.append(down)
    joined = jnp.concatenate(before[::-1] + [total] + after, axis=0)
    return lax.dynamic_slice_in_dim(joined, (n - 1 - me) * rows, n * rows, 0)


def total_of(t, axes):
    return jnp.sum(lax.all_gather(t, axes, axis=0), axis=0)


def per_device(hidden, lengths, norm_gain, w_gate, w_value, w_step, w_state, value_taps, value_shift, state_taps,
               state_shift, step_bias, decay_log, skip_gain, gated_gain, w_output, cotangent):
    row_count = lax.axis_size("row")
    col_count = lax.axis_size("col")
    row, col = lax.axis_index("row"), lax.axis_index("col")
    rows, part = hidden.shape
    tokens = rows * row_count
    seqs = lengths.shape[0]
    heads = step_bias.shape[0]
    inner = value_taps.shape[1]
    head_dim = inner // heads
    sd2 = state_taps.shape[1]
    model = part * col_count
    inner_all = inner * row_count * col_count
    four = row_count == 4
    other = 1 - col

    lens_col = jnp.concatenate([lengths.astype(jnp.int32), col.astype(jnp.int32)[None]])
    channel = lambda v, s: jnp.concatenate([v, s], axis=1)
    pad_s = jnp.zeros((1, sd2), F32)
    pch = jnp.concatenate([
        channel(value_taps, state_taps),
        channel(value_shift[None], state_shift[None]),
        channel(jnp.repeat(skip_gain, head_dim)[None], pad_s),
        channel(gated_gain[None], pad_s),
        jnp.zeros((1, inner + sd2), F32),
    ], axis=0)
    pad_h = lambda v: jnp.pad(v, (0, LANES - heads))[None]
    phd = jnp.concatenate([pad_h(step_bias), pad_h(-jnp.exp(decay_log)), jnp.zeros((6, LANES), F32)], axis=0)
    seg = (jnp.arange(inner)[:, None] // head_dim == jnp.arange(LANES)[None, :]).astype(BF16)
    gain_a = norm_gain[None]
    gain_b = swap_col(gain_a)

    cut = lambda w, c, width: lax.dynamic_slice_in_dim(w, c * width, width, 1)
    step_pad = jnp.zeros((part, LANES - heads), BF16)
    w_small = jnp.concatenate([w_state, cut(w_step, col, heads), step_pad], axis=1)
    w_small_o = jnp.concatenate([w_state, cut(w_step, other, heads), step_pad], axis=1)
    w_small_b = swap_col(w_small_o)
    w_gate_b = swap_col(cut(w_gate, other, inner))
    w_value_b = swap_col(cut(w_value, other, inner))
    w_output_b = swap_col(lax.dynamic_slice_in_dim(w_output, other * inner, inner, 0))

    x_a, x_b = gather_both(hidden, row, four)
    (normed, gate, vpre, vconv, y, spre, sconv, sp, s_in, g, stats) = run_forward(
        heads, lens_col, x_a, x_b, gain_a, gain_b, w_gate, w_gate_b, w_value, w_value_b, w_small, w_small_b, pch, phd, seqs)
    gate_square = total_of(stats[0:1, :], ("row", "col"))
    inv_scale = stats[1:2, :]
    inv_gate = lax.rsqrt(gate_square / inner_all + EPS)

    g_o = swap_col(g)
    cot_a, cot_b = gather_both(cotangent, row, four)
    w_out_own = lax.dynamic_slice_in_dim(w_output, col * inner, inner, 0)
    w_out_other = lax.dynamic_slice_in_dim(w_output, other * inner, inner, 0)
    own_row = lambda t: lax.dynamic_slice_in_dim(t, row * rows, rows, 1)

    def out_part(bits):
        at = (row ^ bits) * rows
        take = lambda t: lax.dynamic_slice_in_dim(t, at, rows, 0)
        return (mm(take(g), w_out_own, NN) + mm(take(g_o), w_out_other, NN)).astype(BF16)

    if four:
        out_own = scatter_four(out_part, rows)
    else:
        out_all = (mm(g, w_out_own, NN) + mm(g_o, w_out_other, NN)).astype(BF16)
        out_own = lax.psum_scatter(out_all, "row", scatter_dimension=0, tiled=True).astype(F32)
    mixed = (hidden.astype(F32) + out_own * own_row(inv_gate).reshape(rows, 1)).astype(BF16)

    bn, stats_b = run_back_norm(col.astype(jnp.int32)[None], cot_a, cot_b, w_output, w_output_b, g)
    cot_n = (cot_a.astype(F32) * inv_gate.reshape(tokens, 1)).astype(BF16)
    grad_out = (mm(g, cot_n, TN), mm(g_o, cot_n, TN))
    gate_total = total_of(stats_b[0:1, :], ("row", "col"))
    c2 = inv_gate**3 * gate_total / inner_all
    rows8 = jnp.concatenate([inv_gate, c2, inv_scale, jnp.zeros((5, tokens), F32)], axis=0)
    dg, dv, ds, pc, ph = run_backward(
        heads, lens_col, rows8, bn, gate, vpre, vconv, y, spre, sconv, sp, s_in, pch, phd, seg, seqs)
    dg_o, dv_o, ds_o = swap_col(dg), swap_col(dv), swap_col(ds)

    def input_part(start, count):
        block = min(BLOCK, count)
        scal = jnp.stack([start // block, col, other]).astype(jnp.int32)
        return run_input_back(scal, count, dg, dg_o, dv, dv_o, ds, ds_o, x_a, gain_a, w_gate, w_value, w_small, w_small_o)

    if four:
        parts = {bits: input_part((row ^ bits) * rows, rows) for bits in (3, 2, 1, 0)}
        input_own = scatter_four(lambda bits: parts[bits][0], rows)
        dots = jnp.zeros((1, tokens), F32)
        for bits in range(4):
            dots = lax.dynamic_update_slice(dots, parts[bits][1][0:1], (0, (row ^ bits) * rows))
        gain_part = sum(parts[bits][2] for bits in range(4))
    else:
        all_part, stats_x, gain_part = input_part(row * 0, tokens)
        input_own = lax.psum_scatter(all_part, "row", scatter_dimension=0, tiled=True).astype(F32)
        dots = stats_x[0:1]
    dot_own = own_row(total_of(dots, ("row", "col"))).reshape(rows, 1)
    scale_own = own_row(inv_scale).reshape(rows, 1)
    grad_hidden = (cotangent.astype(F32) + input_own * norm_gain
                   - (dot_own * scale_own**2 / model) * hidden.astype(F32))
    grad_norm_gain = total_of(jnp.sum(gain_part, axis=0), ("dp", "row"))

    both = (ds[:, :sd2].astype(F32) + ds_o[:, :sd2].astype(F32)).astype(BF16)
    d_small = jnp.concatenate([both, ds[:, sd2:], ds_o[:, sd2:]], axis=1)
    grad_small = mm(normed, d_small, TN)
    order = lambda mine, theirs, axis: jnp.where(
        col == 0, jnp.concatenate([mine, theirs], axis=axis), jnp.concatenate([theirs, mine], axis=axis))
    whole_sum = lambda pair, axis: order(line_sum(pair[0], "dp"), line_sum(pair[1], "dp"), axis).astype(F32)
    grad_w_output = whole_sum(grad_out, 0)
    grad_w_gate = whole_sum((mm(normed, dg, TN), mm(normed, dg_o, TN)), 1)
    grad_w_value = whole_sum((mm(normed, dv, TN), mm(normed, dv_o, TN)), 1)
    grad_w_state = lax.psum(grad_small[:, :sd2].astype(BF16), ("dp", "row")).astype(F32)
    step_own, step_other = grad_small[:, sd2 : sd2 + heads], grad_small[:, sd2 + LANES : sd2 + LANES + heads]
    grad_w_step = order(step_own, step_other, 1)
    pcs = jnp.sum(pc.reshape(7, 8, inner + sd2), axis=1)
    phs = jnp.sum(ph.reshape(2, 8, LANES), axis=1)
    small = jnp.concatenate([pcs[:, :inner].reshape(-1), phs[:, :heads].reshape(-1), grad_w_step.reshape(-1)])
    width = -(-small.shape[0] // (8 * LANES)) * 8
    small = total_of(jnp.pad(small, (0, width * LANES - small.shape[0])).reshape(width, LANES), ("dp",)).reshape(-1)
    pcs_v = small[: 7 * inner].reshape(7, inner)
    phs = small[7 * inner : 7 * inner + 2 * heads].reshape(2, heads)
    grad_w_step = small[7 * inner + 2 * heads : 7 * inner + 2 * heads + part * 2 * heads].reshape(part, 2 * heads)
    pcs_s = total_of(pcs[0:5, inner:], ("dp", "row", "col"))
    grad_skip = jnp.sum(pcs_v[5].reshape(heads, head_dim), axis=1)
    return (
        mixed,
        grad_hidden,
        grad_norm_gain,
        grad_w_gate,
        grad_w_value,
        grad_w_step,
        grad_w_state,
        pcs_v[0:4],
        pcs_v[4],
        pcs_s[0:4],
        pcs_s[4],
        phs[0],
        -jnp.exp(decay_log) * phs[1],
        grad_skip,
        pcs_v[6],
        grad_w_output,
    )


def solution(mesh):
    rows = P(("dp", "row"), "col")
    heads = P(("row", "col"))
    w_in = P("col", "row")
    taps = P(None, ("row", "col"))
    return jax.shard_map(
        per_device,
        mesh=mesh,
        in_specs=(rows, P("dp"), P("col"), w_in, w_in, w_in, P("col", None), taps, heads, P(), P(), heads, heads, heads,
                  heads, P("row", "col"), rows),
        out_specs=(rows, rows, P("col"), w_in, w_in, w_in, P("col", None), taps, heads, P(), P(), heads, heads, heads,
                   heads, P("row", "col")),
        check_vma=False,
    )
```
